512 devices in a mesh: aux: 32 (over z, y_lo), vir: 16 (over x, y_hi, core).
Axes of the slice: x: 4, y: 8 (y_hi: 2, y_lo: 4; y = y_hi * 4 + y_lo), z: 8, core: 2. Of those that a mesh axis runs over, the one named last changes fastest.
Arguments:
- three_index: bfloat16 [8192, 32, 2048], P('aux', None, 'vir'), may hold values from -0.09375 to 0.09375
- trial_vectors: bfloat16 [3, 32, 2048], P(None, None, 'vir'), may hold values from -40 to 40
- occupied_energy: float32 [32], replicated, may hold values from -2 to -0.4
- virtual_energy: float32 [2048], P('vir'), may hold values from 0.4 to 3
Outputs:
- next_vectors: float32 [3, 32, 2048], P(None, None, 'vir')
- rayleigh: float32 [3], replicated
The draws below stay inside these ranges and needn't reach their ends.
All inputs are finite; a program needn't handle non-finite values.
Results may differ from the reference program's by a relative error of at most 0.0019.
Values may be sent and summed in bfloat16 or wider, within the bound.
A program may use at most 128 MiB of HBM per device.

```python
import jax
import jax.numpy as jnp
from jax import lax

AUX_DEV = 256
OCC = 32
NROOT = 3
PRODUCTS = 1
AUX = 8192
VIR = 2048


def draw_trial_vectors(key, part):
    key_base = jax.random.fold_in(key, 11)
    key_values, key_rows, key_cols = jax.random.split(key_base, 3)
    row_scale = jnp.exp(jax.random.uniform(key_rows, (NROOT, OCC, 1), jnp.float32) * jnp.log(10.0))
    col_scale = jnp.exp(jax.random.uniform(key_cols, (1, 1, VIR), jnp.float32) * jnp.log(10.0))
    entries = jax.random.truncated_normal(key_values, -4.0, 4.0, (NROOT, OCC, VIR), jnp.float32)
    return (entries * row_scale * col_scale / 10.0).astype(jnp.bfloat16)


def block_scale(rng, dims, shards, least, high):
    level = 1.0
    for axis_at, shards_of in shards:
        steps = jax.random.uniform(jax.random.fold_in(jax.random.fold_in(rng, 6), axis_at), (shards_of,), jnp.float32, least / len(shards), high / len(shards))
        level = level * jnp.repeat(jnp.exp(steps), dims[axis_at] // shards_of).reshape((-1,) + (1,) * (len(dims) - 1 - axis_at))
    return level


def bell_draw(stream_key, extent, width, bound, cuts=(), dtype=jnp.bfloat16):
    values = jax.random.normal(stream_key, extent, jnp.float32) * width
    if len(cuts) > 0:
        values = block_scale(stream_key, extent, cuts, -0.22, 0.18) * values
    return jnp.clip(values, min=-bound, max=bound).astype(dtype)


def setup_inputs(seed: int = 0) -> dict:
    arg_keys = jax.random.split(jax.random.key(seed), 5)
    return {
        "three_index": bell_draw(arg_keys[0], (AUX, OCC, VIR), (1.0 / (AUX * OCC * VIR) ** 0.25), 0.09375, ((0, 32), (2, 16))),
        "trial_vectors": draw_trial_vectors(jax.random.fold_in(arg_keys[4], 71), 0),
        "occupied_energy": jnp.clip(jax.random.uniform(arg_keys[2], (OCC,), jnp.float32, -2.0, -0.4), -2.0, -0.4),
        "virtual_energy": jnp.clip(0.4 + 2.6 * jax.random.uniform(arg_keys[3], (VIR,), jnp.float32) ** block_scale(arg_keys[3], (VIR,), ((0, 16),), -0.2, 0.2), 0.4, 3.0),
    }


EPS = 1e-06

def hessian_terms(three_index, trial_half):
    blocks = three_index.reshape(AUX // AUX_DEV, AUX_DEV, OCC, VIR)
    trial = trial_half.astype(jnp.float32)

    def absorb(accum, block):
        values = block.astype(jnp.float32)
        fit = jnp.einsum('pia,ria->rp', values, trial)
        fit_round = lax.optimization_barrier(fit.astype(jnp.bfloat16)).astype(jnp.float32)
        pair = jnp.einsum('pib,rjb->pirj', values, trial)
        pair_round = lax.optimization_barrier(pair.astype(jnp.bfloat16)).astype(jnp.float32)
        coulomb = jnp.einsum('rp,pia->ria', fit_round, values)
        exchange_term = jnp.einsum('pirj,pja->ria', pair_round, values)
        return (accum + (2.0 * coulomb - exchange_term), None)
    start_sum = jnp.zeros((NROOT, OCC, VIR), jnp.float32)
    total, _ = lax.scan(absorb, start_sum, blocks)
    return total

def reference(three_index, trial_vectors, occupied_energy, virtual_energy):
    energy_gap = virtual_energy[None, :] - occupied_energy[:, None]
    current = trial_vectors.astype(jnp.float32)
    rayleigh = jnp.zeros((NROOT,), jnp.float32)
    for repeat_index in range(PRODUCTS):
        trial_half = current.astype(jnp.bfloat16)
        total = hessian_terms(three_index, trial_half)
        sigma_full = energy_gap[None] * current + total
        numer = lax.optimization_barrier(jnp.sum(current * sigma_full, axis=(1, 2)))
        denom = lax.optimization_barrier(jnp.sum(current * current, axis=(1, 2))) + EPS
        rayleigh = numer / denom
        stepped = current - (sigma_full - rayleigh[:, None, None] * current) / energy_gap[None]
        square_mean = lax.optimization_barrier(jnp.mean(stepped * stepped, axis=(1, 2)))
        current = stepped * lax.rsqrt(square_mean + EPS)[:, None, None]
    return (current, rayleigh)
```

```python
import functools

import jax
import jax.numpy as jnp
from jax import lax
from jax.experimental import pallas as pl
from jax.experimental.pallas import tpu as pltpu
from jax.sharding import PartitionSpec as P

EPS = 1e-06
MESH = pl.DeviceIdType.MESH
F32, BF16 = jnp.float32, jnp.bfloat16

Z, YL = 8, 4
NV = 16
JOBS = 1


def kernel(
    b_hbm, x_ref, oe_ref, ve_ref, out_ref, rho_ref,
    bfull, xfull, pt, r1, r2, ry, w, s3, r3, r4, fin, r5, s5,
    local_sem, swap_s, swap_r, x1_s, x1_r, x2_s, x2_r, y_s, y_r, ya_s, ya_r, ag_s, ag_r,
    p3_s, p3_r, p4_s, p4_r, p5_s, p5_r, p6_s, p6_r,
):
    aux, vir = lax.axis_index("aux"), lax.axis_index("vir")
    z, yl = aux // YL, aux % YL
    x, yh, c = vir // 4, (vir // 2) % 2, vir % 2
    rows = 96
    nblk, wide = pt.shape[0], pt.shape[3]
    part = rows // Z
    pending = []

    def remote(src, dst, ss, rs, aux_to=None, vir_to=None):
        target = {"aux": aux if aux_to is None else aux_to, "vir": vir if vir_to is None else vir_to}
        return pltpu.make_async_remote_copy(
            src_ref=src, dst_ref=dst, send_sem=ss, recv_sem=rs, device_id=target, device_id_type=MESH
        )

    def send(*args, **kw):
        copy = remote(*args, **kw)
        copy.start()
        pending.append(copy)

    core = vir + 1 - 2 * c
    xa = x + 1 - 2 * (x % 2)
    xb = 3 - x
    dev_a = xa * 4 + yh * 2 + c
    dev_b = xb * 4 + yh * 2 + c
    dev_y = x * 4 + (1 - yh) * 2 + c
    ha, hb = ((x + 1) // 2) % 2, x // 2
    first, second = (dev_a, dev_b), (dev_b, dev_a)
    hf, hg = (ha, hb), (hb, ha)
    own = [4 * h + 2 * hf[h] + hg[h] for h in range(2)]

    lane = pl.ds(pl.multiple_of(c * 128, 128), 128)
    load_b = pltpu.make_async_copy(b_hbm.at[c], bfull.at[:, :, lane], local_sem.at[0])
    load_b.start()
    load_x = pltpu.make_async_copy(x_ref, xfull.at[:, lane], local_sem.at[1])
    load_x.start()
    barrier = pltpu.get_barrier_semaphore()

    def greet(aux_to, vir_to):
        pl.semaphore_signal(barrier, inc=1, device_id={"aux": aux_to, "vir": vir_to}, device_id_type=MESH)

    nzc = 2 * Z
    mine = z * 2 + c

    def zc(t):
        return (t // 2) * YL + yl, vir - c + t % 2

    for d in range(1, NV):
        greet(aux, (vir + d) % NV)
    for d in range(1, nzc):
        greet(*zc((mine + d) % nzc))
    for d in range(1, YL):
        greet(z * YL + (yl + d) % YL, vir)
    pl.semaphore_wait(barrier, NV - 1 + nzc - 1 + YL - 1)

    send(b_hbm.at[1 - c], bfull.at[:, :, lane], swap_s.at[0], swap_r.at[0], vir_to=core)
    send(x_ref, xfull.at[:, lane], swap_s.at[1], swap_r.at[1], vir_to=core)
    load_b.wait()
    load_x.wait()
    for copy in pending:
        copy.wait_recv()

    def pair(k, q):
        rows_of = bfull[k, q * wide:(q + 1) * wide, :]
        pt[k, q] = lax.dot_general(
            xfull[...], rows_of, (((1,), (1,)), ((), ())), preferred_element_type=F32
        )

    lane_id = lax.broadcasted_iota(jnp.int32, (32, 128), 1)
    diagonal = lax.broadcasted_iota(jnp.int32, (32, 128), 0) == lane_id % 32
    slot = lane_id // 32
    ga = lax.broadcasted_iota(jnp.int32, (128, 128), 0) // 32
    gb = lax.broadcasted_iota(jnp.int32, (128, 128), 1) // 32
    groups = (ga == gb).astype(F32)

    def weights(total):
        padded = jnp.concatenate([total, jnp.zeros((128 - rows, wide), F32)], axis=0)
        turned = padded.T
        blocks, diags = [], []
        for g in range(wide // 128):
            src = [turned[(4 * g + s) * 32:(4 * g + s + 1) * 32, :] for s in range(4)]
            for r in range(3):
                moved = [pltpu.roll(src[s], ((s - r) * 32) % 128, 1) if s != r else src[s] for s in range(4)]
                block = jnp.where(
                    slot == 0, moved[0], jnp.where(slot == 1, moved[1], jnp.where(slot == 2, moved[2], moved[3]))
                )
                blocks.append(block)
                diags.append(jnp.sum(jnp.where(diagonal, block, 0.0), axis=0, keepdims=True))
        while len(diags) % 8:
            diags.append(jnp.zeros((1, 128), F32))
        traces = lax.dot_general(
            jnp.concatenate(diags, axis=0), groups, (((1,), (0,)), ((), ())),
            precision=lax.Precision.HIGHEST, preferred_element_type=F32,
        )
        fit = traces.astype(BF16).astype(F32)
        out = {}
        for g in range(wide // 128):
            for r in range(3):
                n = 3 * g + r
                rounded = blocks[n].astype(BF16).astype(F32)
                coulomb = jnp.where(diagonal, 2.0 * fit[n:n + 1, :], 0.0)
                out[r, g] = (coulomb - rounded).astype(BF16)
        return out

    for q in range(JOBS):
        for h in range(2):
            away = 4 * h + 2 * (1 - hf[h])
            for g in range(2):
                pair(away + g, q)
            send(pt.at[pl.ds(away, 2), q], r1.at[h, q], x1_s.at[h, q], x1_r.at[h, q], vir_to=first[h])
        for h in range(2):
            keep = 4 * h + 2 * hf[h]
            for g in range(2):
                pair(keep + g, q)
    for q in range(JOBS):
        for h in range(2):
            keep = 4 * h + 2 * hf[h]
            remote(pt.at[pl.ds(keep, 2), q], r1.at[h, q], x1_s.at[h, q], x1_r.at[h, q], vir_to=first[h]).wait_recv()
            gone = keep + 1 - hg[h]
            pt[gone, q] = pt[gone, q] + r1[h, q, 1 - hg[h]]
            send(pt.at[gone, q], r2.at[h, q], x2_s.at[h, q], x2_r.at[h, q], vir_to=second[h])
            pt[own[h], q] = pt[own[h], q] + r1[h, q, hg[h]]
    k_own = own[0] * (1 - yh) + own[1] * yh
    k_other = own[0] * yh + own[1] * (1 - yh)
    f_own, g_own = dev_a * (1 - yh) + dev_b * yh, dev_b * (1 - yh) + dev_a * yh
    f_other, g_other = g_own, f_own
    for q in range(JOBS):
        for h in range(2):
            remote(pt.at[own[h], q], r2.at[h, q], x2_s.at[h, q], x2_r.at[h, q], vir_to=second[h]).wait_recv()
            pt[own[h], q] = pt[own[h], q] + r2[h, q]
        send(pt.at[k_other, q], ry.at[q], y_s.at[q], y_r.at[q], vir_to=dev_y)
    for q in range(JOBS):
        remote(pt.at[k_other, q], ry.at[q], y_s.at[q], y_r.at[q], vir_to=dev_y).wait_recv()
        for (r, g), value in weights(pt[k_own, q] + ry[q]).items():
            w[k_own, q, r * 32:(r + 1) * 32, g * 128:(g + 1) * 128] = value
        block = w.at[k_own, q]
        send(block, block, ya_s.at[q], ya_r.at[q], vir_to=dev_y)
        send(block, block, ag_s.at[yh, 0, q], ag_r.at[yh, 0, q], vir_to=g_own)
        send(block, block, ag_s.at[yh, 1, q], ag_r.at[yh, 1, q], vir_to=f_own)
    for q in range(JOBS):
        block = w.at[k_other, q]
        remote(block, block, ya_s.at[q], ya_r.at[q], vir_to=dev_y).wait_recv()
        send(block, block, ag_s.at[1 - yh, 0, q], ag_r.at[1 - yh, 0, q], vir_to=g_other)
        send(block, block, ag_s.at[1 - yh, 1, q], ag_r.at[1 - yh, 1, q], vir_to=f_other)
    for q in range(JOBS):
        for h in range(2):
            block = w.at[4 * h + 2 * hf[h] + 1 - hg[h], q]
            remote(block, block, ag_s.at[h, 0, q], ag_r.at[h, 0, q], vir_to=second[h]).wait_recv()
            send(block, block, ag_s.at[h, 2, q], ag_r.at[h, 2, q], vir_to=first[h])
    for q in range(JOBS):
        for h in range(2):
            for n, g in ((1, hg[h]), (2, 1 - hg[h])):
                block = w.at[4 * h + 2 * (1 - hf[h]) + g, q]
                remote(block, block, ag_s.at[h, n, q], ag_r.at[h, n, q], vir_to=first[h]).wait_recv()

    total = jnp.zeros((rows, 256), F32)
    for k in range(nblk):
        for q in range(JOBS):
            total = total + jnp.dot(
                w[k, q], bfull[k, q * wide:(q + 1) * wide, :], preferred_element_type=F32
            )
    for n in range(Z):
        for m in range(2):
            s3[n, m] = total[n * part:(n + 1) * part, m * 128:(m + 1) * 128]

    for d in range(1, nzc):
        t = (mine + d) % nzc
        aux_to, vir_to = zc(t)
        send(s3.at[t // 2, t % 2], r3.at[z, c], p3_s.at[d], p3_r.at[mine], aux_to=aux_to, vir_to=vir_to)
    r3[z, c] = s3[z, c]
    for d in range(1, nzc):
        t = (mine + d) % nzc
        piece = r3.at[t // 2, t % 2]
        remote(piece, piece, p3_s.at[d], p3_r.at[t], vir_to=core).wait_recv()
    piece_sum = jnp.zeros((part, 128), F32)
    for n in range(Z):
        for m in range(2):
            piece_sum = piece_sum + r3[n, m]
    r4[yl] = piece_sum
    for d in range(1, YL):
        send(r4.at[yl], r4.at[yl], p4_s.at[d], p4_r.at[yl], aux_to=z * YL + (yl + d) % YL)
    for d in range(1, YL):
        t = (yl + d) % YL
        remote(r4.at[t], r4.at[t], p4_s.at[d], p4_r.at[t], vir_to=core).wait_recv()
    piece_sum = r4[0]
    for n in range(1, YL):
        piece_sum = piece_sum + r4[n]
    fin[z] = piece_sum
    for d in range(1, Z):
        send(fin.at[z], fin.at[z], p5_s.at[d], p5_r.at[z], aux_to=((z + d) % Z) * YL + yl)
    for d in range(1, Z):
        t = (z + d) % Z
        remote(fin.at[t], fin.at[t], p5_s.at[d], p5_r.at[t], vir_to=core).wait_recv()
    terms = jnp.concatenate([fin[n] for n in range(Z)], axis=0)

    i_row = lax.broadcasted_iota(jnp.int32, (32, 32), 0)
    i_col = lax.broadcasted_iota(jnp.int32, (32, 32), 1)
    occupied = jnp.sum(
        jnp.where(i_row == i_col, jnp.broadcast_to(oe_ref[...], (32, 32)), 0.0), axis=1, keepdims=True
    )
    gap = ve_ref[...] - occupied
    current = x_ref[...].astype(F32)

    def total_of(v):
        return jnp.sum(jnp.sum(v, axis=0, keepdims=True), axis=1, keepdims=True)

    out_lane = lax.broadcasted_iota(jnp.int32, (1, 128), 1)
    message = jnp.zeros((1, 128), F32)
    held = []
    for r in range(3):
        cur = current[r * 32:(r + 1) * 32, :]
        sigma = gap * cur + terms[r * 32:(r + 1) * 32, :]
        numer, denom = total_of(cur * sigma), total_of(cur * cur)
        guess = numer / (denom + EPS)
        base = cur - (sigma - guess * cur) / gap
        slope = cur / gap
        values = (numer, denom, total_of(base * base), total_of(base * slope), total_of(slope * slope))
        for n, v in enumerate(values):
            message = jnp.where(out_lane == 3 * n + r, v, message)
        held.append((cur, sigma))
    r5[vir] = message
    s5[...] = message
    for d in range(1, NV):
        send(s5, r5.at[vir], p6_s.at[d], p6_r.at[vir], vir_to=(vir + d) % NV)
    for d in range(1, NV):
        t = (vir + d) % NV
        remote(s5, r5.at[t], p6_s.at[d], p6_r.at[t], vir_to=core).wait_recv()
    table = jnp.concatenate([r5[n] for n in range(NV)], axis=0)
    table_lane = lax.broadcasted_iota(jnp.int32, (NV, 128), 1)
    entries = 32 * 128 * NV

    def column(n):
        return jnp.sum(jnp.where(table_lane == n, table, 0.0), axis=1, keepdims=True)

    for r in range(3):
        numer, denom, s_0, s_1, s_2 = (column(3 * n + r) for n in range(5))
        guess = numer / (denom + EPS)
        rho = jnp.sum(numer, axis=0, keepdims=True) / (jnp.sum(denom, axis=0, keepdims=True) + EPS)
        shift = rho - guess
        square = jnp.sum(s_0 + shift * (2.0 * s_1 + shift * s_2), axis=0, keepdims=True)
        cur, sigma = held[r]
        stepped = cur - (sigma - rho * cur) / gap
        out_ref[r] = stepped * lax.rsqrt(square / entries + EPS)
        rho_ref[r] = jnp.sum(rho)
    for copy in pending:
        copy.wait_send()


def local(three_index, trial_vectors, occupied_energy, virtual_energy):
    naux, nocc, nvir = three_index.shape
    roots = trial_vectors.shape[0]
    nblk, wide = 8, naux // 16 * nocc // JOBS
    rows = roots * nocc
    dma = pltpu.SemaphoreType.DMA
    vmem = pltpu.VMEM
    return pl.pallas_call(
        kernel,
        out_shape=(
            jax.ShapeDtypeStruct((roots, nocc, nvir), F32),
            jax.ShapeDtypeStruct((roots,), F32),
        ),
        in_specs=[
            pl.BlockSpec(memory_space=pl.ANY),
            pl.BlockSpec(memory_space=vmem),
            pl.BlockSpec(memory_space=vmem),
            pl.BlockSpec(memory_space=vmem),
        ],
        out_specs=(pl.BlockSpec(memory_space=vmem), pl.BlockSpec(memory_space=pltpu.SMEM)),
        scratch_shapes=[
            vmem((nblk, wide * JOBS, 256), BF16),
            vmem((rows, 256), BF16),
            vmem((nblk, JOBS, rows, wide), F32),
            vmem((2, JOBS, 2, rows, wide), F32),
            vmem((2, JOBS, rows, wide), F32),
            vmem((JOBS, rows, wide), F32),
            vmem((nblk, JOBS, rows, wide), BF16),
            vmem((Z, 2, rows // Z, 128), F32),
            vmem((Z, 2, rows // Z, 128), F32),
            vmem((YL, rows // Z, 128), F32),
            vmem((Z, rows // Z, 128), F32),
            vmem((NV, 1, 128), F32),
            vmem((1, 128), F32),
            dma((2,)), dma((2,)), dma((2,)),
            dma((2, JOBS)), dma((2, JOBS)), dma((2, JOBS)), dma((2, JOBS)),
            dma((JOBS,)), dma((JOBS,)), dma((JOBS,)), dma((JOBS,)),
            dma((2, 3, JOBS)), dma((2, 3, JOBS)),
            dma((2 * Z,)), dma((2 * Z,)), dma((YL,)), dma((YL,)), dma((Z,)), dma((Z,)), dma((NV,)), dma((NV,)),
        ],
        compiler_params=pltpu.CompilerParams(collective_id=0, has_side_effects=True, vmem_limit_bytes=40 << 20),
    )(
        three_index.reshape(2, nblk, naux // 16 * nocc, nvir),
        trial_vectors.reshape(rows, nvir),
        occupied_energy.reshape(1, nocc),
        virtual_energy.reshape(1, nvir),
    )


def solution(mesh):
    return jax.shard_map(
        local,
        mesh=mesh,
        in_specs=(P("aux", None, "vir"), P(None, None, "vir"), P(), P("vir")),
        out_specs=(P(None, None, "vir"), P()),
        check_vma=False,
    )
```

```python
import functools

import jax
import jax.numpy as jnp
from jax import lax
from jax.experimental import pallas as pl
from jax.experimental.pallas import tpu as pltpu
from jax.sharding import PartitionSpec as P

EPS = 1e-06
MESH = pl.DeviceIdType.MESH
F32, BF16 = jnp.float32, jnp.bfloat16

Z, YL = 8, 4
NV = 16
JOBS = 4
ORDER = (
    "P0 P1 X0 P2 X1 P3 U0 X2 U1 X3 U2 U3 Y0 Y1 G0 H0 Y2 G1 H1 Y3 F0 G2 H2 F1 G3 H3 F2 F3 T0 T1 T2 T3"
).split()


def kernel(
    b_hbm, x_hbm, oe_hbm, ve_hbm, out_ref, rho_ref,
    bfull, xv, xo, oe, ve, pt, r1, r2, ry, w, acc, cs, cr, r3, r4, fin, r5, s5,
    local_sem, swap_s, swap_r, x1_s, x1_r, x2_s, x2_r, y_s, y_r, ya_s, ya_r, ag_s, ag_r,
    c_s, c_r, p3_s, p3_r, p4_s, p4_r, p5_s, p5_r, p6_s, p6_r, p7_s,
):
    aux, vir = lax.axis_index("aux"), lax.axis_index("vir")
    z, yl = aux // YL, aux % YL
    x, yh, c = vir // 4, (vir // 2) % 2, vir % 2
    rows = 96
    nblk, wide = pt.shape[1], pt.shape[3]
    part = rows // Z
    pending = []

    def remote(src, dst, ss, rs, aux_to=None, vir_to=None):
        target = {"aux": aux if aux_to is None else aux_to, "vir": vir if vir_to is None else vir_to}
        return pltpu.make_async_remote_copy(
            src_ref=src, dst_ref=dst, send_sem=ss, recv_sem=rs, device_id=target, device_id_type=MESH
        )

    def send(*args, **kw):
        copy = remote(*args, **kw)
        copy.start()
        pending.append(copy)
        return copy

    core = vir + 1 - 2 * c
    xa = x + 1 - 2 * (x % 2)
    xb = 3 - x
    dev_a = xa * 4 + yh * 2 + c
    dev_b = xb * 4 + yh * 2 + c
    dev_y = x * 4 + (1 - yh) * 2 + c
    ha, hb = ((x + 1) // 2) % 2, x // 2
    first, second = (dev_a, dev_b), (dev_b, dev_a)
    hf, hg = (ha, hb), (hb, ha)
    own = [4 * h + 2 * hf[h] + hg[h] for h in range(2)]
    pair_xc = x * 2 + c

    def at_xc(t, half):
        return (t // 2) * 4 + half * 2 + t % 2

    lane = pl.ds(pl.multiple_of(c * 128, 128), 128)
    other_lane = pl.ds(pl.multiple_of((1 - c) * 128, 128), 128)
    loads = [
        pltpu.make_async_copy(x_hbm, xv, local_sem.at[0]),
        pltpu.make_async_copy(oe_hbm, oe, local_sem.at[1]),
        pltpu.make_async_copy(ve_hbm, ve, local_sem.at[2]),
    ]
    for q in range(JOBS):
        loads.append(
            pltpu.make_async_copy(
                b_hbm.at[c, :, pl.ds(q * wide, wide), :], bfull.at[q, :, :, lane], local_sem.at[3 + q]
            )
        )
    for copy in loads:
        copy.start()
    barrier = pltpu.get_barrier_semaphore()

    def greet(aux_to, vir_to):
        pl.semaphore_signal(barrier, inc=1, device_id={"aux": aux_to, "vir": vir_to}, device_id_type=MESH)

    near = z * YL + (YL - 1) * (1 - yl // 2)
    far = [z * YL + (2 - 2 * (yl // (YL - 1)) + n) for n in range(2)]
    edge = (yl % (YL - 1)) == 0
    for d in range(1, 8):
        greet(aux, at_xc((pair_xc + d) % 8, yh))
    greet(aux, dev_y)
    for d in range(1, Z):
        greet(((z + d) % Z) * YL + yl, vir)
    for d in range(1, YL):
        greet(z * YL + (yl + d) % YL, vir)
    for t in range(8):
        greet(near, at_xc(t, 1 - yh))
    pl.semaphore_wait(barrier, 7 + 1 + Z - 1 + YL - 1 + jnp.where(edge, 16, 0))

    swaps = [send(x_hbm, xo, swap_s.at[JOBS], swap_r.at[JOBS], vir_to=core)]
    for q in range(JOBS):
        swaps.append(
            send(
                b_hbm.at[1 - c, :, pl.ds(q * wide, wide), :], bfull.at[q, :, :, lane],
                swap_s.at[q], swap_r.at[q], vir_to=core,
            )
        )
    for copy in loads[:4]:
        copy.wait()
    nt = (((1,), (1,)), ((), ()))
    for k in range(nblk):
        pt[0, k] = lax.dot_general(xv[...], bfull[0, k, :, lane], nt, preferred_element_type=F32)
    swaps[0].wait_recv()

    def pair(k, q):
        if q == 0:
            begun = pt[0, k]
        else:
            begun = lax.dot_general(xv[...], bfull[q, k, :, lane], nt, preferred_element_type=F32)
        pt[q, k] = begun + lax.dot_general(xo[...], bfull[q, k, :, other_lane], nt, preferred_element_type=F32)

    lane_id = lax.broadcasted_iota(jnp.int32, (32, 128), 1)
    diagonal = lax.broadcasted_iota(jnp.int32, (32, 128), 0) == lane_id % 32
    slot = lane_id // 32
    ga = lax.broadcasted_iota(jnp.int32, (128, 128), 0) // 32
    gb = lax.broadcasted_iota(jnp.int32, (128, 128), 1) // 32
    groups = (ga == gb).astype(F32)

    def weights(total):
        padded = jnp.concatenate([total, jnp.zeros((128 - rows, 128), F32)], axis=0)
        turned = padded.T
        src = [turned[s * 32:(s + 1) * 32, :] for s in range(4)]
        blocks, diags = [], []
        for r in range(3):
            moved = [pltpu.roll(src[s], ((s - r) * 32) % 128, 1) if s != r else src[s] for s in range(4)]
            block = jnp.where(
                slot == 0, moved[0], jnp.where(slot == 1, moved[1], jnp.where(slot == 2, moved[2], moved[3]))
            )
            blocks.append(block)
            diags.append(jnp.sum(jnp.where(diagonal, block, 0.0), axis=0, keepdims=True))
        traces = lax.dot_general(
            jnp.concatenate(diags + [jnp.zeros((5, 128), F32)], axis=0), groups, (((1,), (0,)), ((), ())),
            precision=lax.Precision.HIGHEST, preferred_element_type=F32,
        )
        fit = traces.astype(BF16).astype(F32)
        out = []
        for r in range(3):
            rounded = blocks[r].astype(BF16).astype(F32)
            coulomb = jnp.where(diagonal, 2.0 * fit[r:r + 1, :], 0.0)
            out.append((coulomb - rounded).astype(BF16))
        return out

    k_own = own[0] * (1 - yh) + own[1] * yh
    k_other = own[0] * yh + own[1] * (1 - yh)
    f_own, g_own = dev_a * (1 - yh) + dev_b * yh, dev_b * (1 - yh) + dev_a * yh
    f_other, g_other = g_own, f_own
    from_g_own = k_own + 1 - 2 * (k_own % 2)
    from_g_other = k_other + 1 - 2 * (k_other % 2)

    def stage_p(q):
        if q:
            loads[3 + q].wait()
        swaps[1 + q].wait_recv()
        for h in range(2):
            away = 4 * h + 2 * (1 - hf[h])
            for g in range(2):
                pair(away + g, q)
            send(pt.at[q, pl.ds(away, 2)], r1.at[h, q], x1_s.at[h, q], x1_r.at[h, q], vir_to=first[h])
        for h in range(2):
            for g in range(2):
                pair(4 * h + 2 * hf[h] + g, q)

    def stage_x(q):
        for h in range(2):
            keep = 4 * h + 2 * hf[h]
            remote(pt.at[q, pl.ds(keep, 2)], r1.at[h, q], x1_s.at[h, q], x1_r.at[h, q], vir_to=first[h]).wait_recv()
            gone = keep + 1 - hg[h]
            pt[q, gone] = pt[q, gone] + r1[h, q, 1 - hg[h]]
            send(pt.at[q, gone], r2.at[h, q], x2_s.at[h, q], x2_r.at[h, q], vir_to=second[h])
        for h in range(2):
            pt[q, own[h]] = pt[q, own[h]] + r1[h, q, hg[h]]

    def stage_u(q):
        for h in range(2):
            remote(pt.at[q, own[h]], r2.at[h, q], x2_s.at[h, q], x2_r.at[h, q], vir_to=second[h]).wait_recv()
            pt[q, own[h]] = pt[q, own[h]] + r2[h, q]
        send(pt.at[q, k_other], ry.at[q], y_s.at[q], y_r.at[q], vir_to=dev_y)

    def stage_y(q):
        remote(pt.at[q, k_other], ry.at[q], y_s.at[q], y_r.at[q], vir_to=dev_y).wait_recv()
        for r, value in enumerate(weights(pt[q, k_own] + ry[q])):
            w[q, k_own, r * 32:(r + 1) * 32, :] = value
        block = w.at[q, k_own]
        send(block, block, ya_s.at[q], ya_r.at[q], vir_to=dev_y)
        send(block, block, ag_s.at[yh, 0, q], ag_r.at[yh, 0, q], vir_to=g_own)
        send(block, block, ag_s.at[yh, 1, q], ag_r.at[yh, 1, q], vir_to=f_own)

    def stage_g(q):
        block = w.at[q, from_g_own]
        remote(block, block, ag_s.at[yh, 0, q], ag_r.at[yh, 0, q], vir_to=g_own).wait_recv()
        send(block, block, ag_s.at[yh, 2, q], ag_r.at[yh, 2, q], vir_to=f_own)

    def stage_h(q):
        block = w.at[q, k_other]
        remote(block, block, ya_s.at[q], ya_r.at[q], vir_to=dev_y).wait_recv()
        send(block, block, ag_s.at[1 - yh, 0, q], ag_r.at[1 - yh, 0, q], vir_to=g_other)
        send(block, block, ag_s.at[1 - yh, 1, q], ag_r.at[1 - yh, 1, q], vir_to=f_other)

    def stage_f(q):
        block = w.at[q, from_g_other]
        remote(block, block, ag_s.at[1 - yh, 0, q], ag_r.at[1 - yh, 0, q], vir_to=g_other).wait_recv()
        send(block, block, ag_s.at[1 - yh, 2, q], ag_r.at[1 - yh, 2, q], vir_to=f_other)

    def stage_t(q):
        for h in range(2):
            for n, g in ((1, hg[h]), (2, 1 - hg[h])):
                block = w.at[q, 4 * h + 2 * (1 - hf[h]) + g]
                remote(block, block, ag_s.at[h, n, q], ag_r.at[h, n, q], vir_to=first[h]).wait_recv()
        total = acc[...] if q else jnp.zeros((rows, 256), F32)
        for k in range(nblk):
            total = total + jnp.dot(w[q, k], bfull[q, k], preferred_element_type=F32)
        acc[...] = total

    stages = {"P": stage_p, "X": stage_x, "U": stage_u, "Y": stage_y, "G": stage_g, "H": stage_h, "F": stage_f, "T": stage_t}
    for step in ORDER:
        stages[step[0]](int(step[1:]))

    for n in range(Z):
        cs[n] = acc[n * part:(n + 1) * part, other_lane]
    give = send(cs, cr, c_s.at[0], c_r.at[0], vir_to=core)
    for n in range(Z):
        r4[n] = acc[n * part:(n + 1) * part, lane]
    give.wait_recv()
    cr[...] = cr[...] + r4[...]
    for d in range(1, Z):
        t = (z + d) % Z
        send(cr.at[t], r3.at[z], p3_s.at[d], p3_r.at[z], aux_to=t * YL + yl)
    r3[z] = cr[z]
    for d in range(1, Z):
        t = (z + d) % Z
        remote(cr.at[t], r3.at[t], p3_s.at[d], p3_r.at[t], vir_to=core).wait_recv()
    piece_sum = r3[0]
    for n in range(1, Z):
        piece_sum = piece_sum + r3[n]
    r5[yl] = piece_sum
    for d in range(1, YL):
        send(r5.at[yl], r5.at[yl], p4_s.at[d], p4_r.at[yl], aux_to=z * YL + (yl + d) % YL)
    for d in range(1, YL):
        t = (yl + d) % YL
        remote(r5.at[t], r5.at[t], p4_s.at[d], p4_r.at[t], vir_to=core).wait_recv()
    piece_sum = r5[0]
    for n in range(1, YL):
        piece_sum = piece_sum + r5[n]
    fin[z] = piece_sum
    for d in range(1, Z):
        send(fin.at[z], fin.at[z], p5_s.at[d], p5_r.at[z], aux_to=((z + d) % Z) * YL + yl)

    i_row = lax.broadcasted_iota(jnp.int32, (32, 32), 0)
    i_col = lax.broadcasted_iota(jnp.int32, (32, 32), 1)
    occupied = jnp.sum(
        jnp.where(i_row == i_col, jnp.broadcast_to(oe[...], (32, 32)), 0.0), axis=1, keepdims=True
    )
    gap = ve[...] - occupied
    current = xv[...].astype(F32)
    for d in range(1, Z):
        t = (z + d) % Z
        remote(fin.at[t], fin.at[t], p5_s.at[d], p5_r.at[t], vir_to=core).wait_recv()
    terms = jnp.concatenate([fin[n] for n in range(Z)], axis=0)

    def total_of(v):
        return jnp.sum(jnp.sum(v, axis=0, keepdims=True), axis=1, keepdims=True)

    out_lane = lax.broadcasted_iota(jnp.int32, (1, 128), 1)
    message = jnp.zeros((1, 128), F32)
    held = []
    for r in range(3):
        cur = current[r * 32:(r + 1) * 32, :]
        sigma = gap * cur + terms[r * 32:(r + 1) * 32, :]
        numer, denom = total_of(cur * sigma), total_of(cur * cur)
        guess = numer / (denom + EPS)
        base = cur - (sigma - guess * cur) / gap
        slope = cur / gap
        values = (numer, denom, total_of(base * base), total_of(base * slope), total_of(slope * slope))
        for n, v in enumerate(values):
            message = jnp.where(out_lane == 3 * n + r, v, message)
        held.append((cur, sigma))
    mine = yh * 8 + pair_xc
    s5[mine] = message
    for d in range(1, 8):
        t = (pair_xc + d) % 8
        send(s5.at[mine], s5.at[mine], p6_s.at[d], p6_r.at[mine], vir_to=at_xc(t, yh))

    @pl.when(edge)
    def _():
        across = [
            remote(
                s5.at[mine], s5.at[mine], p7_s.at[n * 8 + t], p6_r.at[mine],
                aux_to=far[n], vir_to=at_xc(t, 1 - yh),
            )
            for n in range(2)
            for t in range(8)
        ]
        for copy in across:
            copy.start()
        for copy in across:
            copy.wait_send()

    for d in range(1, 8):
        t = yh * 8 + (pair_xc + d) % 8
        remote(s5.at[t], s5.at[t], p6_s.at[d], p6_r.at[t], vir_to=core).wait_recv()
    for d in range(8):
        t = (1 - yh) * 8 + d
        remote(s5.at[t], s5.at[t], p6_s.at[d], p6_r.at[t], vir_to=core).wait_recv()
    table = jnp.concatenate([s5[n] for n in range(NV)], axis=0)
    table_lane = lax.broadcasted_iota(jnp.int32, (NV, 128), 1)
    entries = 32 * 128 * NV

    def column(n):
        return jnp.sum(jnp.where(table_lane == n, table, 0.0), axis=1, keepdims=True)

    for r in range(3):
        numer, denom, s_0, s_1, s_2 = (column(3 * n + r) for n in range(5))
        guess = numer / (denom + EPS)
        rho = jnp.sum(numer, axis=0, keepdims=True) / (jnp.sum(denom, axis=0, keepdims=True) + EPS)
        shift = rho - guess
        square = jnp.sum(s_0 + shift * (2.0 * s_1 + shift * s_2), axis=0, keepdims=True)
        cur, sigma = held[r]
        stepped = cur - (sigma - rho * cur) / gap
        out_ref[r] = stepped * lax.rsqrt(square / entries + EPS)
        rho_ref[r] = jnp.sum(rho)
    for copy in pending:
        copy.wait_send()


def local(three_index, trial_vectors, occupied_energy, virtual_energy):
    naux, nocc, nvir = three_index.shape
    roots = trial_vectors.shape[0]
    nblk, deep = 8, naux // 16 * nocc
    wide = deep // JOBS
    rows = roots * nocc
    dma = pltpu.SemaphoreType.DMA
    vmem = pltpu.VMEM
    hbm = pl.BlockSpec(memory_space=pltpu.HBM)
    return pl.pallas_call(
        kernel,
        out_shape=(
            jax.ShapeDtypeStruct((roots, nocc, nvir), F32),
            jax.ShapeDtypeStruct((roots,), F32),
        ),
        in_specs=[hbm] * 4,
        out_specs=(pl.BlockSpec(memory_space=vmem), pl.BlockSpec(memory_space=pltpu.SMEM)),
        scratch_shapes=[
            vmem((JOBS, nblk, wide, 256), BF16),
            vmem((rows, 128), BF16), vmem((rows, 128), BF16), vmem((1, nocc), F32), vmem((1, nvir), F32),
            vmem((JOBS, nblk, rows, wide), F32),
            vmem((2, JOBS, 2, rows, wide), F32),
            vmem((2, JOBS, rows, wide), F32),
            vmem((JOBS, rows, wide), F32),
            vmem((JOBS, nblk, rows, wide), BF16),
            vmem((rows, 256), F32),
            vmem((Z, rows // Z, 128), F32), vmem((Z, rows // Z, 128), F32),
            vmem((Z, rows // Z, 128), F32), vmem((Z, rows // Z, 128), F32), vmem((Z, rows // Z, 128), F32),
            vmem((YL, rows // Z, 128), F32),
            vmem((NV, 1, 128), F32),
            dma((3 + JOBS,)), dma((JOBS + 1,)), dma((JOBS + 1,)),
            dma((2, JOBS)), dma((2, JOBS)), dma((2, JOBS)), dma((2, JOBS)),
            dma((JOBS,)), dma((JOBS,)), dma((JOBS,)), dma((JOBS,)),
            dma((2, 3, JOBS)), dma((2, 3, JOBS)),
            dma((1,)), dma((1,)), dma((Z,)), dma((Z,)), dma((YL,)), dma((YL,)), dma((Z,)), dma((Z,)),
            dma((8,)), dma((NV,)), dma((16,)),
        ],
        compiler_params=pltpu.CompilerParams(collective_id=0, has_side_effects=True, vmem_limit_bytes=67000000),
    )(
        three_index.reshape(2, nblk, deep, nvir),
        trial_vectors.reshape(rows, nvir),
        occupied_energy.reshape(1, nocc),
        virtual_energy.reshape(1, nvir),
    )


def solution(mesh):
    return jax.shard_map(
        local,
        mesh=mesh,
        in_specs=(P("aux", None, "vir"), P(None, None, "vir"), P(), P("vir")),
        out_specs=(P(None, None, "vir"), P()),
        check_vma=False,
    )
```

```python
import functools

import jax
import jax.numpy as jnp
from jax import lax
from jax.experimental import pallas as pl
from jax.experimental.pallas import tpu as pltpu
from jax.sharding import PartitionSpec as P

EPS = 1e-06
MESH = pl.DeviceIdType.MESH
F32, BF16 = jnp.float32, jnp.bfloat16

Z, YL = 8, 4
NV = 16
JOBS = 4
BOTH = (0, 1, 2, 3)
ORDER = (
    "P0", "P1", "X0", "P2", "X1", "P3", "U0", "X2", "U1", "X3", "U2", "U3", "Y0", "H0", "Y1", "H1",
    "G0", "F0", "Y2", "H2", "G1", "F1", "T0", "Y3", "H3", "G2", "F2", "T1", "G3", "F3", "T2", "T3",
)


def kernel(
    b_hbm, x_hbm, oe_hbm, ve_hbm, out_ref, rho_ref,
    bfull, xv, xo, oe, ve, pt, r1, r2, ry, rz, w, acc, cs, cr, r3, r4, fin, r5, s5,
    local_sem, swap_s, swap_r, x1_s, x1_r, x2_s, x2_r, y_s, y_r, ya_s, ya_r, ag_s, ag_r,
    c_s, c_r, p3_s, p3_r, p4_s, p4_r, p5_s, p5_r, p6_s, p6_r, p7_s,
):
    aux, vir = lax.axis_index("aux"), lax.axis_index("vir")
    z, yl = aux // YL, aux % YL
    x, yh, c = vir // 4, (vir // 2) % 2, vir % 2
    rows = 96
    nblk, wide = pt.shape[1], pt.shape[3]
    part = rows // Z
    pending = []

    def remote(src, dst, ss, rs, aux_to=None, vir_to=None):
        target = {"aux": aux if aux_to is None else aux_to, "vir": vir if vir_to is None else vir_to}
        return pltpu.make_async_remote_copy(
            src_ref=src, dst_ref=dst, send_sem=ss, recv_sem=rs, device_id=target, device_id_type=MESH
        )

    def send(*args, **kw):
        copy = remote(*args, **kw)
        copy.start()
        pending.append(copy)
        return copy

    core = vir + 1 - 2 * c
    xa = x + 1 - 2 * (x % 2)
    xb = 3 - x
    dev_a = xa * 4 + yh * 2 + c
    dev_b = xb * 4 + yh * 2 + c
    dev_y = x * 4 + (1 - yh) * 2 + c
    ha, hb = ((x + 1) // 2) % 2, x // 2
    first, second = (dev_a, dev_b), (dev_b, dev_a)
    hf, hg = (ha, hb), (hb, ha)
    own = [4 * h + 2 * hf[h] + hg[h] for h in range(2)]
    pair_xc = x * 2 + c

    def at_xc(t, half):
        return (t // 2) * 4 + half * 2 + t % 2

    lane = pl.ds(pl.multiple_of(c * 128, 128), 128)
    other_lane = pl.ds(pl.multiple_of((1 - c) * 128, 128), 128)
    loads = [
        pltpu.make_async_copy(x_hbm, xv, local_sem.at[0]),
        pltpu.make_async_copy(oe_hbm, oe, local_sem.at[1]),
        pltpu.make_async_copy(ve_hbm, ve, local_sem.at[2]),
    ]
    for q in range(JOBS):
        loads.append(
            pltpu.make_async_copy(
                b_hbm.at[c, :, pl.ds(q * wide, wide), :], bfull.at[q, :, :, lane], local_sem.at[3 + q]
            )
        )
    for copy in loads:
        copy.start()
    barrier = pltpu.get_barrier_semaphore()

    def greet(aux_to, vir_to):
        pl.semaphore_signal(barrier, inc=1, device_id={"aux": aux_to, "vir": vir_to}, device_id_type=MESH)

    near = z * YL + (YL - 1) * (1 - yl // 2)
    far = [z * YL + (2 - 2 * (yl // (YL - 1)) + n) for n in range(2)]
    edge = (yl % (YL - 1)) == 0
    for d in range(1, 8):
        greet(aux, at_xc((pair_xc + d) % 8, yh))
    greet(aux, dev_y)
    for d in range(1, Z):
        greet(((z + d) % Z) * YL + yl, vir)
    for d in range(1, YL):
        greet(z * YL + (yl + d) % YL, vir)
    for t in range(8):
        greet(near, at_xc(t, 1 - yh))
    pl.semaphore_wait(barrier, 7 + 1 + Z - 1 + YL - 1 + jnp.where(edge, 16, 0))

    swaps = [send(x_hbm, xo, swap_s.at[JOBS], swap_r.at[JOBS], vir_to=core)]
    for q in range(JOBS):
        swaps.append(
            send(
                b_hbm.at[1 - c, :, pl.ds(q * wide, wide), :], bfull.at[q, :, :, lane],
                swap_s.at[q], swap_r.at[q], vir_to=core,
            )
        )
    for copy in loads[:4]:
        copy.wait()
    nt = (((1,), (1,)), ((), ()))
    for k in range(nblk):
        pt[0, k] = lax.dot_general(xv[...], bfull[0, k, :, lane], nt, preferred_element_type=F32)
    swaps[0].wait_recv()

    def pair(k, q):
        if q == 0:
            begun = pt[0, k]
        else:
            begun = lax.dot_general(xv[...], bfull[q, k, :, lane], nt, preferred_element_type=F32)
        pt[q, k] = begun + lax.dot_general(xo[...], bfull[q, k, :, other_lane], nt, preferred_element_type=F32)

    lane_id = lax.broadcasted_iota(jnp.int32, (32, 128), 1)
    diagonal = lax.broadcasted_iota(jnp.int32, (32, 128), 0) == lane_id % 32
    slot = lane_id // 32
    ga = lax.broadcasted_iota(jnp.int32, (128, 128), 0) // 32
    gb = lax.broadcasted_iota(jnp.int32, (128, 128), 1) // 32
    groups = (ga == gb).astype(F32)

    def weights(total):
        padded = jnp.concatenate([total, jnp.zeros((128 - rows, 128), F32)], axis=0)
        turned = padded.T
        src = [turned[s * 32:(s + 1) * 32, :] for s in range(4)]
        blocks, diags = [], []
        for r in range(3):
            moved = [pltpu.roll(src[s], ((s - r) * 32) % 128, 1) if s != r else src[s] for s in range(4)]
            block = jnp.where(
                slot == 0, moved[0], jnp.where(slot == 1, moved[1], jnp.where(slot == 2, moved[2], moved[3]))
            )
            blocks.append(block)
            diags.append(jnp.sum(jnp.where(diagonal, block, 0.0), axis=0, keepdims=True))
        traces = lax.dot_general(
            jnp.concatenate(diags + [jnp.zeros((5, 128), F32)], axis=0), groups, (((1,), (0,)), ((), ())),
            precision=lax.Precision.HIGHEST, preferred_element_type=F32,
        )
        fit = traces.astype(BF16).astype(F32)
        out = []
        for r in range(3):
            rounded = blocks[r].astype(BF16).astype(F32)
            coulomb = jnp.where(diagonal, 2.0 * fit[r:r + 1, :], 0.0)
            out.append((coulomb - rounded).astype(BF16))
        return out

    k_own = own[0] * (1 - yh) + own[1] * yh
    k_other = own[0] * yh + own[1] * (1 - yh)
    f_own, g_own = dev_a * (1 - yh) + dev_b * yh, dev_b * (1 - yh) + dev_a * yh
    f_other, g_other = g_own, f_own
    from_g_own = k_own + 1 - 2 * (k_own % 2)
    from_g_other = k_other + 1 - 2 * (k_other % 2)

    def stage_p(q):
        if q:
            loads[3 + q].wait()
        swaps[1 + q].wait_recv()
        for h in range(2):
            away = 4 * h + 2 * (1 - hf[h])
            for g in range(2):
                pair(away + g, q)
            send(pt.at[q, pl.ds(away, 2)], r1.at[h, q], x1_s.at[h, q], x1_r.at[h, q], vir_to=first[h])
        for h in range(2):
            for g in range(2):
                pair(4 * h + 2 * hf[h] + g, q)

    def stage_x(q):
        for h in range(2):
            keep = 4 * h + 2 * hf[h]
            remote(pt.at[q, pl.ds(keep, 2)], r1.at[h, q], x1_s.at[h, q], x1_r.at[h, q], vir_to=first[h]).wait_recv()
            gone = keep + 1 - hg[h]
            pt[q, gone] = pt[q, gone] + r1[h, q, 1 - hg[h]]
            send(pt.at[q, gone], r2.at[h, q], x2_s.at[h, q], x2_r.at[h, q], vir_to=second[h])
        for h in range(2):
            pt[q, own[h]] = pt[q, own[h]] + r1[h, q, hg[h]]

    def stage_u(q):
        for h in range(2):
            remote(pt.at[q, own[h]], r2.at[h, q], x2_s.at[h, q], x2_r.at[h, q], vir_to=second[h]).wait_recv()
            pt[q, own[h]] = pt[q, own[h]] + r2[h, q]
        send(pt.at[q, k_other], ry.at[q], y_s.at[q], y_r.at[q], vir_to=dev_y)
        if q in BOTH:
            send(pt.at[q, k_own], rz.at[q], ya_s.at[q], ya_r.at[q], vir_to=dev_y)

    def put_weights(q, k, received):
        for r, value in enumerate(weights(pt[q, k] + received)):
            w[q, k, r * 32:(r + 1) * 32, :] = value

    def stage_y(q):
        remote(pt.at[q, k_other], ry.at[q], y_s.at[q], y_r.at[q], vir_to=dev_y).wait_recv()
        put_weights(q, k_own, ry[q])
        block = w.at[q, k_own]
        if q not in BOTH:
            send(block, block, ya_s.at[q], ya_r.at[q], vir_to=dev_y)
        send(block, block, ag_s.at[yh, 0, q], ag_r.at[yh, 0, q], vir_to=g_own)
        send(block, block, ag_s.at[yh, 1, q], ag_r.at[yh, 1, q], vir_to=f_own)

    def stage_g(q):
        block = w.at[q, from_g_own]
        remote(block, block, ag_s.at[yh, 0, q], ag_r.at[yh, 0, q], vir_to=g_own).wait_recv()
        send(block, block, ag_s.at[yh, 2, q], ag_r.at[yh, 2, q], vir_to=f_own)

    def stage_h(q):
        block = w.at[q, k_other]
        if q in BOTH:
            remote(pt.at[q, k_own], rz.at[q], ya_s.at[q], ya_r.at[q], vir_to=dev_y).wait_recv()
            put_weights(q, k_other, rz[q])
        else:
            remote(block, block, ya_s.at[q], ya_r.at[q], vir_to=dev_y).wait_recv()
        send(block, block, ag_s.at[1 - yh, 0, q], ag_r.at[1 - yh, 0, q], vir_to=g_other)
        send(block, block, ag_s.at[1 - yh, 1, q], ag_r.at[1 - yh, 1, q], vir_to=f_other)

    def stage_f(q):
        block = w.at[q, from_g_other]
        remote(block, block, ag_s.at[1 - yh, 0, q], ag_r.at[1 - yh, 0, q], vir_to=g_other).wait_recv()
        send(block, block, ag_s.at[1 - yh, 2, q], ag_r.at[1 - yh, 2, q], vir_to=f_other)

    def stage_t(q):
        for h in range(2):
            for n, g in ((1, hg[h]), (2, 1 - hg[h])):
                block = w.at[q, 4 * h + 2 * (1 - hf[h]) + g]
                remote(block, block, ag_s.at[h, n, q], ag_r.at[h, n, q], vir_to=first[h]).wait_recv()
        total = acc[...] if q else jnp.zeros((rows, 256), F32)
        for k in range(nblk):
            total = total + jnp.dot(w[q, k], bfull[q, k], preferred_element_type=F32)
        acc[...] = total

    stages = {"P": stage_p, "X": stage_x, "U": stage_u, "Y": stage_y, "G": stage_g, "H": stage_h, "F": stage_f, "T": stage_t}
    for step in ORDER:
        stages[step[0]](int(step[1:]))

    for n in range(Z):
        cs[n] = acc[n * part:(n + 1) * part, other_lane]
    give = send(cs, cr, c_s.at[0], c_r.at[0], vir_to=core)
    for n in range(Z):
        r4[n] = acc[n * part:(n + 1) * part, lane]
    give.wait_recv()
    cr[...] = cr[...] + r4[...]
    for d in range(1, Z):
        t = (z + d) % Z
        send(cr.at[t], r3.at[z], p3_s.at[d], p3_r.at[z], aux_to=t * YL + yl)
    r3[z] = cr[z]
    for d in range(1, Z):
        t = (z + d) % Z
        remote(cr.at[t], r3.at[t], p3_s.at[d], p3_r.at[t], vir_to=core).wait_recv()
    piece_sum = r3[0]
    for n in range(1, Z):
        piece_sum = piece_sum + r3[n]
    r5[yl] = piece_sum
    for d in range(1, YL):
        send(r5.at[yl], r5.at[yl], p4_s.at[d], p4_r.at[yl], aux_to=z * YL + (yl + d) % YL)
    for d in range(1, YL):
        t = (yl + d) % YL
        remote(r5.at[t], r5.at[t], p4_s.at[d], p4_r.at[t], vir_to=core).wait_recv()
    piece_sum = r5[0]
    for n in range(1, YL):
        piece_sum = piece_sum + r5[n]
    fin[z] = piece_sum
    for d in range(1, Z):
        send(fin.at[z], fin.at[z], p5_s.at[d], p5_r.at[z], aux_to=((z + d) % Z) * YL + yl)

    i_row = lax.broadcasted_iota(jnp.int32, (32, 32), 0)
    i_col = lax.broadcasted_iota(jnp.int32, (32, 32), 1)
    occupied = jnp.sum(
        jnp.where(i_row == i_col, jnp.broadcast_to(oe[...], (32, 32)), 0.0), axis=1, keepdims=True
    )
    gap = ve[...] - occupied
    current = xv[...].astype(F32)

    out_lane = lax.broadcasted_iota(jnp.int32, (8, 128), 1)
    out_row = lax.broadcasted_iota(jnp.int32, (8, 128), 0)

    def lanes_of(parts, at):
        fill = [jnp.zeros((1, 128), F32)] * (8 - len(parts))
        sums = jnp.sum(jnp.concatenate([jnp.sum(v, axis=0, keepdims=True) for v in parts] + fill, axis=0), axis=1, keepdims=True)
        return sums, jnp.sum(jnp.where(out_lane == out_row + at, sums, 0.0), axis=0, keepdims=True)

    cur = [current[r * 32:(r + 1) * 32, :] for r in range(3)]
    slope = [v / gap for v in cur]
    early, early_row = lanes_of([v * v for v in cur] + [v * v for v in slope], 0)
    for d in range(1, Z):
        t = (z + d) % Z
        remote(fin.at[t], fin.at[t], p5_s.at[d], p5_r.at[t], vir_to=core).wait_recv()
    terms = jnp.concatenate([fin[n] for n in range(Z)], axis=0)
    sigma = [gap * cur[r] + terms[r * 32:(r + 1) * 32, :] for r in range(3)]
    cross, cross_row = lanes_of([cur[r] * sigma[r] for r in range(3)], 6)
    guess = cross / (early + EPS)
    base = [cur[r] - (sigma[r] - guess[r:r + 1, :] * cur[r]) / gap for r in range(3)]
    _, late_row = lanes_of([v * v for v in base] + [base[r] * slope[r] for r in range(3)], 9)
    message = early_row + cross_row + late_row
    mine = yh * 8 + pair_xc
    s5[mine] = message
    for d in range(1, 8):
        t = (pair_xc + d) % 8
        send(s5.at[mine], s5.at[mine], p6_s.at[d], p6_r.at[mine], vir_to=at_xc(t, yh))

    @pl.when(edge)
    def _():
        across = [
            remote(
                s5.at[mine], s5.at[mine], p7_s.at[n * 8 + t], p6_r.at[mine],
                aux_to=far[n], vir_to=at_xc(t, 1 - yh),
            )
            for n in range(2)
            for t in range(8)
        ]
        for copy in across:
            copy.start()
        for copy in across:
            copy.wait_send()

    for d in range(1, 8):
        t = yh * 8 + (pair_xc + d) % 8
        remote(s5.at[t], s5.at[t], p6_s.at[d], p6_r.at[t], vir_to=core).wait_recv()
    for d in range(8):
        t = (1 - yh) * 8 + d
        remote(s5.at[t], s5.at[t], p6_s.at[d], p6_r.at[t], vir_to=core).wait_recv()
    table = jnp.concatenate([s5[n] for n in range(NV)], axis=0)
    entries = 32 * 128 * NV

    def column(v, n):
        return pltpu.roll(v, 128 - n, 1) if n else v

    denom, numer = table, column(table, 6)
    guess = numer / (denom + EPS)
    rho = jnp.sum(numer, axis=0, keepdims=True) / (jnp.sum(denom, axis=0, keepdims=True) + EPS)
    shift = rho - guess
    square = jnp.sum(
        column(table, 9) + shift * (2.0 * column(table, 12) + shift * column(table, 3)), axis=0, keepdims=True
    )
    scale = lax.rsqrt(square / entries + EPS)
    for r in range(3):
        rho_r = rho[:, r:r + 1]
        stepped = cur[r] - (sigma[r] - rho_r * cur[r]) / gap
        out_ref[r] = stepped * scale[:, r:r + 1]
        rho_ref[r] = jnp.sum(rho_r)
    for copy in pending:
        copy.wait_send()


def local(three_index, trial_vectors, occupied_energy, virtual_energy):
    naux, nocc, nvir = three_index.shape
    roots = trial_vectors.shape[0]
    nblk, deep = 8, naux // 16 * nocc
    wide = deep // JOBS
    rows = roots * nocc
    dma = pltpu.SemaphoreType.DMA
    vmem = pltpu.VMEM
    hbm = pl.BlockSpec(memory_space=pltpu.HBM)
    return pl.pallas_call(
        kernel,
        out_shape=(
            jax.ShapeDtypeStruct((roots, nocc, nvir), F32),
            jax.ShapeDtypeStruct((roots,), F32),
        ),
        in_specs=[hbm] * 4,
        out_specs=(pl.BlockSpec(memory_space=vmem), pl.BlockSpec(memory_space=pltpu.SMEM)),
        scratch_shapes=[
            vmem((JOBS, nblk, wide, 256), BF16),
            vmem((rows, 128), BF16), vmem((rows, 128), BF16), vmem((1, nocc), F32), vmem((1, nvir), F32),
            vmem((JOBS, nblk, rows, wide), F32),
            vmem((2, JOBS, 2, rows, wide), F32),
            vmem((2, JOBS, rows, wide), F32),
            vmem((JOBS, rows, wide), F32), vmem((JOBS, rows, wide), F32),
            vmem((JOBS, nblk, rows, wide), BF16),
            vmem((rows, 256), F32),
            vmem((Z, rows // Z, 128), F32), vmem((Z, rows // Z, 128), F32),
            vmem((Z, rows // Z, 128), F32), vmem((Z, rows // Z, 128), F32), vmem((Z, rows // Z, 128), F32),
            vmem((YL, rows // Z, 128), F32),
            vmem((NV, 1, 128), F32),
            dma((3 + JOBS,)), dma((JOBS + 1,)), dma((JOBS + 1,)),
            dma((2, JOBS)), dma((2, JOBS)), dma((2, JOBS)), dma((2, JOBS)),
            dma((JOBS,)), dma((JOBS,)), dma((JOBS,)), dma((JOBS,)),
            dma((2, 3, JOBS)), dma((2, 3, JOBS)),
            dma((1,)), dma((1,)), dma((Z,)), dma((Z,)), dma((YL,)), dma((YL,)), dma((Z,)), dma((Z,)),
            dma((8,)), dma((NV,)), dma((16,)),
        ],
        compiler_params=pltpu.CompilerParams(collective_id=0, has_side_effects=True, vmem_limit_bytes=67000000),
    )(
        three_index.reshape(2, nblk, deep, nvir),
        trial_vectors.reshape(rows, nvir),
        occupied_energy.reshape(1, nocc),
        virtual_energy.reshape(1, nvir),
    )


def solution(mesh):
    return jax.shard_map(
        local,
        mesh=mesh,
        in_specs=(P("aux", None, "vir"), P(None, None, "vir"), P(), P("vir")),
        out_specs=(P(None, None, "vir"), P()),
        check_vma=False,
    )
```
